32 devices in a mesh: dp: 4 (over z), ctx: 4 (over x, core), tp: 2 (over y).
Axes of the slice: x: 2, y: 2, z: 4, core: 2. Of those that a mesh axis runs over, the one named last changes fastest.
Arguments:
- hidden: bfloat16 [12288, 768], P(('dp', 'ctx', 'tp')), may hold values from -6 to 6
- grad_output: bfloat16 [4096, 2048], P(('dp', 'ctx', 'tp')), may hold values from -6 to 6
- expert_ids: int32 [4096, 2], P(('dp', 'ctx', 'tp')), may hold values from 0 to 7, all different within a row; in each aligned block of 128 rows (0 to 127, 128 to 255, ...) at most 48 rows name the same one
- gate_weights: float32 [4096, 2], P(('dp', 'ctx', 'tp')), may hold values from 0.2 to 1
- w_down: bfloat16 [8, 768, 2048], P(('ctx', 'tp')), may hold values from -0.21875 to 0.21875
Outputs:
- combined: bfloat16 [4096, 2048], P(('dp', 'ctx', 'tp'))
- grad_hidden: bfloat16 [12288, 768], P(('dp', 'ctx', 'tp'))
- grad_down: bfloat16 [8, 768, 2048], P(('ctx', 'tp'), 'dp')
The draws below stay inside these ranges and needn't reach their ends.
Inputs may be any that keep to these rules, and one draw needn't show every extreme that they name: `expert_ids`: each row names 2 different experts. Among the 128 rows of one device no expert is named more than 48 times, and in every draw some device names some expert exactly 48 times.
All inputs are finite; a program needn't handle non-finite values.
Results may differ from the reference program's by a relative error of at most 0.017.
Values may be sent and summed in bfloat16 or wider, within the bound.
No kernel may reach another device: no remote copies, remote signals or barrier semaphores. Data moves between devices by JAX's collectives and lax.ppermute only.
A program may use at most 64 MiB of HBM per device.

```python
import math
import jax
import jax.numpy as jnp
import numpy as np
from jax import lax

D = 2048
FF = 768
TOPK = 2
TOK_DEV = 128
EXPERTS = 8
CAP = 48
TOKENS = 4096
N_DP = 4
DEVICES = 32


def raised(drawn, stream_key, source, target, parts, factor):
    owner, partner = [(jnp.arange(drawn.shape[axis_at]) // (drawn.shape[axis_at] // parts)).reshape([-1 if axis == axis_at else 1 for axis in range(drawn.ndim)]) for axis_at in (source, target)]
    chosen = jax.random.permutation(stream_key, parts)[partner]
    strong = (owner == chosen) | (owner == (partner + parts // 2) % parts)
    return jnp.where(strong, factor * drawn, drawn)


def level_of(own_key, dims, cuts, low, largest):
    level, own = 1.0, jax.random.fold_in(own_key, 6)
    for position, blocks in cuts:
        draws = jnp.exp(jax.random.uniform(jax.random.fold_in(own, position), (blocks,), jnp.float32, low / len(cuts), largest / len(cuts)))
        level = level * jnp.repeat(draws, dims[position] // blocks).reshape([-1 if axis == position else 1 for axis in range(len(dims))])
    return level


def shared_out(stream_key, own, number, rows, count, top, limit, lean):
    order = jax.random.permutation(stream_key, count)
    heavy_load, common = portions_of(count, rows * top, limit, lean, True), portions_of(count, rows * top, limit, lean, False)
    places = jnp.arange(count)

    def named(sizes, turn):
        used = int((sizes > 0).sum())
        fixed = max(1, used // 4)
        shifted = fixed + (places - fixed + turn * (used - fixed)) % max(1, count - fixed)
        return jnp.zeros((count,), jnp.int32).at[order[jnp.where(places < fixed, places, shifted)]].set(jnp.asarray(sizes, jnp.int32))

    sizes = jnp.where(number % 4 == 0, named(heavy_load, number // 4), named(common, number - number // 4 - 1))
    mixed = jax.random.permutation(jax.random.fold_in(own, 3), count)
    source_of, taker = mixed[0:count // 2 * 2:2], mixed[1:count // 2 * 2:2]
    margin = jnp.minimum(sizes[source_of] - 1, limit - sizes[taker]) // 2
    margin = jnp.where((source_of == order[0]) | (taker == order[0]) | (sizes[taker] == 0), 0, jnp.maximum(margin, 0))
    shifted = jax.random.randint(jax.random.fold_in(own, 4), (count // 2,), 0, 1 << 20) % (margin + 1)
    sizes = sizes.at[source_of].add(-shifted).at[taker].add(shifted)
    members = jnp.searchsorted(jnp.cumsum(sizes), jnp.arange(rows * top), side="right").astype(jnp.int32)
    table = members.reshape(top, rows).T
    table = table[jax.random.permutation(jax.random.fold_in(own, 1), rows)]
    turn = jax.random.randint(jax.random.fold_in(own, 2), (rows, 1), 0, top)
    return jnp.take_along_axis(table, (jnp.arange(top)[None, :] + turn) % top, axis=1)


def portions_of(number_of, total, bound, lean, full):
    loads = [(1 << 20) // math.isqrt(grade ** lean) + 1 for grade in range(1, number_of + 1)]
    largest = bound if full else min(bound, max(-(-total // number_of), total * loads[0] // sum(loads)))
    least = 1 if total - largest >= number_of - 1 else 0
    given, rest = [largest] + [least] * (number_of - 1), total - largest - least * (number_of - 1)
    while rest > 0:
        movable = [i for i in range(1, number_of) if given[i] < largest] or [i for i in range(1, number_of) if given[i] < bound]
        pool, budget = sum([loads[i] for i in movable]), rest
        for i in movable:
            extra = min(bound - given[i], max(1, budget * loads[i] // pool), rest)
            given[i] = given[i] + extra
            rest = rest - extra
    return np.array(given)


def normal_values(stream_key, shape, width, reach, cuts=(), kind=jnp.bfloat16):
    factor_of = level_of(stream_key, shape, cuts, -0.22, 0.18) if cuts else 1.0
    values = jax.random.normal(stream_key, shape, jnp.float32) * width * factor_of
    return jnp.minimum(jnp.maximum(values, -reach), reach).astype(kind)


def heavy_noise(key, extent, deviation, bound, cuts, heavy, kind=jnp.bfloat16):
    result = deviation * jax.random.normal(key, extent, jnp.float32)
    if cuts:
        result = result * level_of(key, extent, cuts, -0.22, 0.18)
    return jnp.clip(raised(result, jax.random.fold_in(key, 3), *heavy), -bound, bound).astype(kind)


def setup_inputs(seed: int = 0) -> dict:
    keys = jax.random.split(jax.random.key(seed), 6)
    hidden = heavy_noise(keys[0], (DEVICES * EXPERTS * CAP, FF), 1.0, 6.0, ((0, 32),), (0, 1, 32, 2.75))
    grad_output = normal_values(keys[1], (TOKENS, D), 1.0, 6.0, ((0, 32),))
    expert_ids_keys = jax.random.split(jax.random.fold_in(keys[2], 1), TOKENS // TOK_DEV)
    expert_ids_turns = jax.random.permutation(jax.random.fold_in(keys[2], 3), TOKENS // TOK_DEV)
    expert_ids = jax.vmap(lambda own, number: shared_out(jax.random.fold_in(keys[2], 2), own, number, TOK_DEV, EXPERTS, TOPK, CAP, 2))(expert_ids_keys, expert_ids_turns).reshape((TOKENS, TOPK))
    gate_weights = jnp.clip(0.2 + 0.8 * jax.random.uniform(keys[3], (TOKENS, TOPK), jnp.float32) ** level_of(keys[3], (TOKENS, TOPK), ((0, 32),), -0.2, 0.2), 0.2, 1.0)
    w_down = normal_values(keys[4], (EXPERTS, FF, D), FF ** -0.5, 0.21875, ((0, 8),))
    return {"hidden": hidden, "grad_output": grad_output, "expert_ids": expert_ids, "gate_weights": gate_weights, "w_down": w_down}


grad_scale = 0.015625


def slot_index(ids_block):
    flat_ids = ids_block.reshape(-1).astype(jnp.int32)
    one_hot = (flat_ids[:, None] == jnp.arange(EXPERTS, dtype=jnp.int32)[None, :]).astype(jnp.int32)
    earlier = jnp.cumsum(one_hot, axis=0) - one_hot
    ranking = jnp.sum(earlier * one_hot, axis=1)
    return (flat_ids * CAP + ranking).astype(jnp.int32)


def expert_forward(operands):
    rows, matrix = operands
    return jnp.dot(rows, matrix, preferred_element_type=jnp.float32).astype(jnp.bfloat16)


def expert_backward(operands):
    rows, matrix, grads = operands
    grad_rows = lax.dot_general(grads, matrix, (((1,), (1,)), ((), ())), preferred_element_type=jnp.float32).astype(jnp.bfloat16)
    weight_part = lax.dot_general(rows, grads, (((0,), (0,)), ((), ())), preferred_element_type=jnp.float32)
    weight_part = lax.optimization_barrier(weight_part.astype(jnp.bfloat16)).astype(jnp.float32)
    return grad_rows, weight_part


def take_rows(table, positions):
    return table[positions]


def place_rows(positions, values):
    return jnp.zeros((EXPERTS * CAP, D), values.dtype).at[positions].set(values)


def make_group(w_down):
    def per_group(summed, inputs):
        hidden_group, grad_group, ids_group, gate_group = inputs
        positions = jax.vmap(slot_index)(ids_group)
        expert_out = lax.map(expert_forward, (hidden_group, w_down))
        by_source = expert_out.reshape(EXPERTS, EXPERTS, CAP, D).transpose(1, 0, 2, 3).reshape(EXPERTS, EXPERTS * CAP, D)
        picked = jax.vmap(take_rows)(by_source, positions).astype(jnp.float32).reshape(EXPERTS, TOK_DEV, TOPK, D)
        combined = jnp.sum(gate_group[..., None] * picked, axis=2).astype(jnp.bfloat16)
        scaled = (gate_group[..., None] * grad_group[:, :, None, :].astype(jnp.float32)).astype(jnp.bfloat16)
        scaled = scaled.reshape(EXPERTS, TOK_DEV * TOPK, D)
        outgoing = jax.vmap(place_rows)(positions, scaled)
        incoming = outgoing.reshape(EXPERTS, EXPERTS, CAP, D).transpose(1, 0, 2, 3).reshape(EXPERTS, EXPERTS * CAP, D)
        grad_rows, weight_part = lax.map(expert_backward, (hidden_group, w_down, incoming))
        return summed + weight_part, (combined, grad_rows)
    return per_group


def reference(hidden, grad_output, expert_ids, gate_weights, w_down):
    hidden_groups = hidden.reshape(N_DP, EXPERTS, EXPERTS * CAP, FF)
    grad_groups = grad_output.reshape(N_DP, EXPERTS, TOK_DEV, D)
    id_groups = expert_ids.reshape(N_DP, EXPERTS, TOK_DEV, TOPK)
    gate_groups = gate_weights.reshape(N_DP, EXPERTS, TOK_DEV, TOPK)
    zero_sum = jnp.zeros((EXPERTS, FF, D), jnp.float32)
    summed, (combined, grad_rows) = lax.scan(make_group(w_down), zero_sum, (hidden_groups, grad_groups, id_groups, gate_groups))
    grad_down = (summed * grad_scale).astype(jnp.bfloat16)
    return combined.reshape(grad_output.shape), grad_rows.reshape(hidden.shape), grad_down
```

```python
import jax
import jax.numpy as jnp
from jax import lax
from jax.experimental import pallas as pl
from jax.experimental.pallas import tpu as pltpu
from jax.sharding import PartitionSpec as P

grad_scale = 0.015625
PIECES = 4
F32 = jnp.float32
BF16 = jnp.bfloat16


def call(body, outs, ins, name, flops=0, smem=0):
    moved = sum(a.size * a.dtype.itemsize for a in (*ins, *outs))
    in_specs = [
        pl.BlockSpec(memory_space=pltpu.SMEM if i < smem else pltpu.VMEM) for i in range(len(ins))
    ]
    return pl.pallas_call(
        body,
        out_shape=tuple(outs),
        in_specs=in_specs,
        out_specs=tuple(pl.BlockSpec(memory_space=pltpu.VMEM) for _ in outs),
        name=name,
        cost_estimate=pl.CostEstimate(flops=flops, bytes_accessed=moved, transcendentals=0),
        compiler_params=pltpu.CompilerParams(vmem_limit_bytes=24 * 2**20),
    )(*ins)


def iota(shape, axis):
    return lax.broadcasted_iota(jnp.int32, shape, axis)


def slot_rows(ids, experts, capacity):
    choices, tokens = ids.shape
    named = [(iota((experts, tokens), 0) == ids[k : k + 1]).astype(F32) for k in range(choices)]
    before = (iota((tokens, tokens), 0) < iota((tokens, tokens), 1)).astype(BF16)
    earlier = jnp.dot(sum(named).astype(BF16), before, preferred_element_type=F32)
    slots = []
    for k in range(choices):
        rank = jnp.sum(named[k] * earlier, axis=0, keepdims=True)
        slots.append(ids[k : k + 1] * capacity + rank.astype(jnp.int32))
        earlier = earlier + named[k]
    return slots


def dispatch(ids, gates, grads, experts, capacity, widths):
    choices, tokens = ids.shape
    rows = experts * capacity

    def body(ids_ref, gates_ref, grads_ref, *out_refs):
        slots = slot_rows(ids_ref[...], experts, capacity)
        pick = jnp.zeros((rows, tokens), F32)
        scale = jnp.zeros((rows, 1), F32)
        for k in range(choices):
            hit = iota((rows, tokens), 0) == slots[k]
            pick = pick + hit.astype(F32)
            scale = scale + jnp.sum(jnp.where(hit, gates_ref[k : k + 1, :], 0.0), axis=1, keepdims=True)
        pick = pick.astype(BF16)
        start = 0
        for ref, width in zip(out_refs, widths):
            chosen = jnp.dot(pick, grads_ref[:, start : start + width], preferred_element_type=F32)
            ref[...] = (chosen * scale).astype(BF16)
            start += width

    return call(
        body,
        [jax.ShapeDtypeStruct((rows, w), BF16) for w in widths],
        [ids, gates, grads],
        "dispatch",
        2 * rows * tokens * sum(widths),
    )


def combine(ids, gates, returned, experts, capacity):
    choices, tokens = ids.shape
    rows, width = returned.shape

    def body(ids_ref, gates_ref, returned_ref, out_ref):
        slots = slot_rows(ids_ref[...], experts, capacity)
        same = iota((tokens, tokens), 0) == iota((tokens, tokens), 1)
        picks, scales = [], []
        for k in range(choices):
            slot = jnp.sum(jnp.where(same, slots[k], 0), axis=1, keepdims=True)
            picks.append((iota((tokens, rows), 1) == slot).astype(F32).astype(BF16))
            scales.append(jnp.sum(jnp.where(same, gates_ref[k : k + 1, :], 0.0), axis=1, keepdims=True))
        step = min(512, width)
        for start in range(0, width, step):
            block = returned_ref[:, start : start + step]
            out_ref[:, start : start + step] = sum(
                jnp.dot(p, block, preferred_element_type=F32) * s for p, s in zip(picks, scales)
            ).astype(BF16)

    return call(
        body,
        [jax.ShapeDtypeStruct((tokens, width), BF16)],
        [ids, gates, returned],
        "combine",
        2 * choices * rows * tokens * width,
    )[0]


def grad_rows(pieces, weight):
    rows, hidden_units = pieces[0].shape[0], weight.shape[0]

    def body(weight_ref, *refs):
        *piece_refs, out_ref = refs
        total, start = None, 0
        for ref in piece_refs:
            width = ref.shape[1]
            part = lax.dot_general(
                ref[...],
                weight_ref[:, start : start + width],
                (((1,), (1,)), ((), ())),
                preferred_element_type=F32,
            )
            total = part if total is None else total + part
            start += width
        out_ref[...] = total.astype(BF16)

    return call(
        body,
        [jax.ShapeDtypeStruct((rows, hidden_units), BF16)],
        [weight, *pieces],
        "grad_rows",
        2 * rows * weight.size,
    )[0]


def exchange(x, experts):
    shaped = x.reshape(experts, -1, x.shape[1])
    return lax.all_to_all(shaped, ("ctx", "tp"), split_axis=0, concat_axis=0, tiled=True).reshape(x.shape)


def folded_parts(side, mine, theirs, piece, piece_theirs):
    half, width = mine.shape[1] // 2, piece.shape[1]

    def body(side_ref, mine_ref, theirs_ref, piece_ref, piece_theirs_ref, give_ref, keep_ref):
        def rows(which):
            columns = pl.ds(pl.multiple_of(which * half, half), half)
            return sum(
                lax.dot_general(h[:, columns], p[...], (((0,), (0,)), ((), ())), preferred_element_type=F32)
                for h, p in ((mine_ref, piece_ref), (theirs_ref, piece_theirs_ref))
            )

        give_ref[...] = rows(1 - side_ref[0]).astype(BF16)
        keep_ref[...] = rows(side_ref[0])

    return call(
        body,
        [jax.ShapeDtypeStruct((half, width), BF16), jax.ShapeDtypeStruct((half, width), F32)],
        [side, mine, theirs, piece, piece_theirs],
        "folded_parts",
        8 * mine.shape[0] * half * width,
        smem=1,
    )


def finish(side, keep, got):
    half, width = keep.shape
    share = half // 2

    def body(side_ref, keep_ref, got_ref, own_ref, give_ref):
        def rows(which):
            at = pl.ds(pl.multiple_of(which * share, share), share)
            return ((keep_ref[at, :] + got_ref[at, :].astype(F32)) * grad_scale).astype(BF16)

        give_ref[...] = rows(side_ref[0])
        own_ref[...] = rows(1 - side_ref[0])

    return call(
        body,
        [jax.ShapeDtypeStruct((share, width), BF16)] * 2,
        [side, keep, got],
        "finish",
        smem=1,
    )


def local(hidden, grad_output, expert_ids, gate_weights, w_down):
    replicas = lax.axis_size("dp")
    experts = lax.axis_size("ctx") * lax.axis_size("tp")
    capacity = hidden.shape[0] // experts
    width = grad_output.shape[1]
    weight = w_down[0]
    ids, gates = expert_ids.T, gate_weights.T
    widths = [width // PIECES] * PIECES

    outgoing = dispatch(ids, gates, grad_output, experts, capacity, widths)
    pieces = [exchange(x, experts) for x in outgoing]
    if replicas == 4:
        place = lax.axis_index("dp")
        side = (place // 2).reshape(1)
        at_end = (place == 0) | (place == replicas - 1)
        fold, swap, back = [(0, 1), (3, 2)], [(1, 2), (2, 1)], [(1, 0), (2, 3)]
        theirs = lax.ppermute(hidden, "dp", fold)
        shares = []
        for piece in pieces:
            give, keep = folded_parts(side, hidden, theirs, piece, lax.ppermute(piece, "dp", fold))
            own, give = finish(side, keep, lax.ppermute(give, "dp", swap))
            shares.append(jnp.where(at_end, lax.ppermute(give, "dp", back), own))
        grad_down = jnp.concatenate(shares, axis=1)
    else:
        incoming = jnp.concatenate(pieces, axis=1)
        part = lax.dot_general(hidden, incoming, (((0,), (0,)), ((), ())), preferred_element_type=F32)
        summed = lax.psum_scatter(part.astype(BF16), "dp", scatter_dimension=0, tiled=True)
        grad_down = (summed.astype(F32) * grad_scale).astype(BF16)

    expert_out = jnp.dot(hidden, weight, preferred_element_type=F32).astype(BF16)
    returned = exchange(expert_out, experts)
    combined = combine(ids, gates, returned, experts, capacity)
    grad_hidden = grad_rows(pieces, weight)
    return (combined, grad_hidden, grad_down[None])


def solution(mesh):
    rows = P(("dp", "ctx", "tp"), None)
    return jax.shard_map(
        local,
        mesh=mesh,
        in_specs=(rows, rows, rows, rows, P(("ctx", "tp"), None, None)),
        out_specs=(rows, rows, P(("ctx", "tp"), "dp", None)),
        check_vma=False,
    )
```

```python
import jax
import jax.numpy as jnp
from jax import lax
from jax.experimental import pallas as pl
from jax.experimental.pallas import tpu as pltpu
from jax.sharding import PartitionSpec as P

grad_scale = 0.015625
PARTS = ((4,), (6, 6))
F32 = jnp.float32
BF16 = jnp.bfloat16
GROUP = ("ctx", "tp")


def call(body, outs, ins, name, flops=0, smem=0, scratch=(), in_hbm=(), out_hbm=()):
    in_specs = [
        pl.BlockSpec(memory_space=pltpu.SMEM if i < smem else pltpu.HBM if i in in_hbm else pltpu.VMEM)
        for i in range(len(ins))
    ]
    return pl.pallas_call(
        body,
        out_shape=tuple(outs),
        in_specs=in_specs,
        out_specs=tuple(
            pl.BlockSpec(memory_space=pltpu.HBM if i in out_hbm else pltpu.VMEM) for i in range(len(outs))
        ),
        scratch_shapes=scratch,
        name=name,
        cost_estimate=pl.CostEstimate(flops=0, bytes_accessed=0, transcendentals=0),
        compiler_params=pltpu.CompilerParams(vmem_limit_bytes=14 * 2**20),
    )(*ins)


def like(shape, dtype=BF16):
    return jax.ShapeDtypeStruct(shape, dtype)


def iota(shape, axis):
    return lax.broadcasted_iota(jnp.int32, shape, axis)


def after(x, *others):
    return lax.optimization_barrier((x, others))[0]


def exchange(x, experts):
    shaped = x.reshape(experts, -1, x.shape[1])
    return lax.all_to_all(shaped, GROUP, split_axis=0, concat_axis=0, tiled=True).reshape(x.shape)


def slot_rows(ids, experts, capacity):
    choices, tokens = ids.shape
    named = [(iota((experts, tokens), 0) == ids[k : k + 1]).astype(F32) for k in range(choices)]
    before = (iota((tokens, tokens), 0) < iota((tokens, tokens), 1)).astype(BF16)
    earlier = jnp.dot(sum(named).astype(BF16), before, preferred_element_type=F32)
    slots = []
    for k in range(choices):
        rank = jnp.sum(named[k] * earlier, axis=0, keepdims=True)
        slots.append(ids[k : k + 1] * capacity + rank.astype(jnp.int32))
        earlier = earlier + named[k]
    return slots


def dispatch(ids, gates, grads, experts, capacity, widths):
    choices, tokens = ids.shape
    rows = experts * capacity

    def body(ids_hbm, gates_hbm, grads_hbm, *refs):
        *out_refs, ids_ref, gates_ref, grads_ref, sems = refs
        copies = [
            pltpu.make_async_copy(src, dst, sems.at[i])
            for i, (src, dst) in enumerate(
                ((ids_hbm, ids_ref), (gates_hbm, gates_ref), (grads_hbm, grads_ref))
            )
        ]
        for copy in copies:
            copy.start()
        copies[0].wait()
        slots = slot_rows(ids_ref[...], experts, capacity)
        copies[1].wait()
        pick = jnp.zeros((rows, tokens), F32)
        scale = jnp.zeros((rows, 1), F32)
        for k in range(choices):
            hit = iota((rows, tokens), 0) == slots[k]
            pick = pick + hit.astype(F32)
            scale = scale + jnp.sum(jnp.where(hit, gates_ref[k : k + 1, :], 0.0), axis=1, keepdims=True)
        pick = pick.astype(BF16)
        copies[2].wait()
        start = 0
        for ref, width in zip(out_refs, widths):
            chosen = jnp.dot(pick, grads_ref[:, start : start + width], preferred_element_type=F32)
            ref[...] = (chosen * scale).astype(BF16)
            start += width

    return call(
        body,
        [like((rows, w)) for w in widths],
        [ids, gates, grads],
        "dispatch",
        2 * rows * tokens * sum(widths),
        in_hbm=(0, 1, 2),
        scratch=[
            pltpu.VMEM(ids.shape, ids.dtype),
            pltpu.VMEM(gates.shape, gates.dtype),
            pltpu.VMEM(grads.shape, grads.dtype),
            pltpu.SemaphoreType.DMA((3,)),
        ],
    )


def combine(ids, gates, returned, experts, capacity):
    choices, tokens = ids.shape
    rows, width = returned.shape

    def body(ids_ref, gates_ref, returned_ref, out_ref):
        slots = slot_rows(ids_ref[...], experts, capacity)
        same = iota((tokens, tokens), 0) == iota((tokens, tokens), 1)
        picks, scales = [], []
        for k in range(choices):
            slot = jnp.sum(jnp.where(same, slots[k], 0), axis=1, keepdims=True)
            picks.append((iota((tokens, rows), 1) == slot).astype(F32).astype(BF16))
            scales.append(jnp.sum(jnp.where(same, gates_ref[k : k + 1, :], 0.0), axis=1, keepdims=True))
        step = min(512, width)
        for start in range(0, width, step):
            block = returned_ref[:, start : start + step]
            out_ref[:, start : start + step] = sum(
                jnp.dot(p, block, preferred_element_type=F32) * s for p, s in zip(picks, scales)
            ).astype(BF16)

    return call(
        body,
        [like((tokens, width))],
        [ids, gates, returned],
        "combine",
        2 * choices * rows * tokens * width,
    )[0]


def expert_rows(rows, weight):
    width = weight.shape[1]
    step = min(512, width)

    def body(rows_ref, weight_ref, out_hbm, out_ref, sems):
        copies = []
        for i, start in enumerate(range(0, width, step)):
            columns = slice(start, start + step)
            out_ref[:, columns] = jnp.dot(
                rows_ref[...], weight_ref[:, columns], preferred_element_type=F32
            ).astype(BF16)
            copies.append(pltpu.make_async_copy(out_ref.at[:, columns], out_hbm.at[:, columns], sems.at[i]))
            copies[-1].start()
        for copy in copies:
            copy.wait()

    out = like((rows.shape[0], width))
    return call(
        body,
        [out],
        [rows, weight],
        "expert_rows",
        2 * rows.shape[0] * weight.size,
        out_hbm=(0,),
        scratch=[pltpu.VMEM(out.shape, out.dtype), pltpu.SemaphoreType.DMA((width // step,))],
    )[0]


def grad_rows(pieces, weight):
    rows, hidden_units = pieces[0].shape[0], weight.shape[0]

    def body(weight_ref, *refs):
        *piece_refs, out_ref = refs
        total, start = None, 0
        for ref in piece_refs:
            width = ref.shape[1]
            part = lax.dot_general(
                ref[...],
                weight_ref[:, start : start + width],
                (((1,), (1,)), ((), ())),
                preferred_element_type=F32,
            )
            total = part if total is None else total + part
            start += width
        out_ref[...] = total.astype(BF16)

    return call(
        body,
        [like((rows, hidden_units))],
        [weight, *pieces],
        "grad_rows",
        2 * rows * weight.size,
    )[0]


def folded_parts(spot, mine, theirs, piece, piece_theirs):
    half, width = mine.shape[1] // 2, piece.shape[1]

    def body(spot_ref, mine_ref, theirs_ref, piece_ref, piece_theirs_ref, give_ref, keep_hbm, keep_ref, sem):
        def rows(which):
            columns = pl.ds(pl.multiple_of(which * half, half), half)
            return sum(
                lax.dot_general(h[:, columns], p[...], (((0,), (0,)), ((), ())), preferred_element_type=F32)
                for h, p in ((mine_ref, piece_ref), (theirs_ref, piece_theirs_ref))
            )

        keep_ref[...] = rows(spot_ref[0]).astype(BF16)
        copy = pltpu.make_async_copy(keep_ref, keep_hbm, sem)
        copy.start()
        give_ref[...] = rows(1 - spot_ref[0]).astype(BF16)
        copy.wait()

    return call(
        body,
        [like((half, width))] * 2,
        [spot, mine, theirs, piece, piece_theirs],
        "folded_parts",
        8 * mine.shape[0] * half * width,
        smem=1,
        out_hbm=(1,),
        scratch=[pltpu.VMEM((half, width), BF16), pltpu.SemaphoreType.DMA],
    )


def finish(spot, keep, got):
    half, width = keep.shape
    share = half // 2

    def body(spot_ref, keep_ref, got_ref, own_ref, give_ref):
        def rows(which):
            at = pl.ds(pl.multiple_of(which * share, share), share)
            return ((keep_ref[at, :].astype(F32) + got_ref[at, :].astype(F32)) * grad_scale).astype(BF16)

        give_ref[...] = rows(spot_ref[0])
        own_ref[...] = rows(1 - spot_ref[0])

    return call(body, [like((share, width))] * 2, [spot, keep, got], "finish", smem=1)


def shares(spot, own, handed):
    rows, width = own[0].shape[0], sum(x.shape[1] for x in own)

    def body(spot_ref, *refs):
        *in_refs, out_ref = refs
        at_end, start = spot_ref[1] != 0, 0
        for own_ref, handed_ref in zip(in_refs[: len(own)], in_refs[len(own) :]):
            columns = slice(start, start + own_ref.shape[1])
            out_ref[:, columns] = jnp.where(at_end, handed_ref[...], own_ref[...])
            start += own_ref.shape[1]

    return call(body, [like((rows, width))], [spot, *own, *handed], "shares", smem=1)[0]


def local(hidden, grad_output, expert_ids, gate_weights, w_down):
    replicas = lax.axis_size("dp")
    experts = lax.axis_size("ctx") * lax.axis_size("tp")
    capacity = hidden.shape[0] // experts
    width = grad_output.shape[1]
    weight = w_down[0]
    ids, gates = expert_ids.T, gate_weights.T
    widths = [[p * width // 16 for p in cuts] for cuts in PARTS]
    line = replicas == 4
    fold, swap, back = [(0, 1), (3, 2)], [(1, 2), (2, 1)], [(1, 0), (2, 3)]

    theirs = lax.ppermute(hidden, "dp", fold) if line else hidden
    outgoing = dispatch(ids, gates, grad_output, experts, capacity, [sum(w) for w in widths])
    expert_out = expert_rows(hidden, weight)
    if not line:
        pieces = [exchange(x, experts) for x in outgoing]
        returned = exchange(expert_out, experts)
        incoming = jnp.concatenate(pieces, axis=1)
        part = lax.dot_general(hidden, incoming, (((0,), (0,)), ((), ())), preferred_element_type=F32)
        summed = lax.psum_scatter(part.astype(BF16), "dp", scatter_dimension=0, tiled=True)
        grad_down = (summed.astype(F32) * grad_scale).astype(BF16)
        combined = combine(ids, gates, returned, experts, capacity)
        return (combined, grad_rows(pieces, weight), grad_down[None])

    place = lax.axis_index("dp")
    at_end = (place == 0) | (place == replicas - 1)
    spot = jnp.stack([(2 * place >= replicas).astype(jnp.int32), at_end.astype(jnp.int32)])

    first = exchange(outgoing[0], experts)
    pieces, folded = [first], [lax.ppermute(first, "dp", fold)]
    give, keep = folded_parts(spot, hidden, theirs, pieces[0], folded[0])
    gives, keeps = [give], [keep]
    arrived = after(exchange(after(outgoing[1], expert_out, theirs), experts), give)
    start = 0
    for cut in widths[1]:
        pieces.append(arrived[:, start : start + cut])
        folded.append(lax.ppermute(pieces[-1], "dp", fold))
        start += cut
    last = len(pieces) - 1
    got = [lax.ppermute(give, "dp", swap)]
    returned = exchange(after(expert_out, pieces[-1], give), experts)
    folded[1] = after(folded[1], got[0])
    for i in range(1, last + 1):
        give, keep = folded_parts(spot, hidden, theirs, pieces[i], folded[i])
        gives.append(give)
        keeps.append(keep)
        got.append(lax.ppermute(give, "dp", swap))

    got[:last] = after(tuple(got[:last]), gives[-1])
    grad_hidden = grad_rows(list(after(tuple(pieces), gives[-1])), weight)
    got[-1] = after(got[-1], grad_hidden)
    formed, handed = [], []
    for i in range(last + 1):
        own, give = finish(spot, keeps[i], got[i])
        formed.append(own)
        handed.append(lax.ppermute(give, "dp", back))
        if i < last:
            got[-1] = after(got[-1], handed[-1])
    combined = combine(ids, gates, returned, experts, capacity)
    grad_down = shares(spot, formed, handed)
    return (combined, grad_hidden, grad_down[None])


def solution(mesh):
    rows = P(("dp", "ctx", "tp"), None)
    return jax.shard_map(
        local,
        mesh=mesh,
        in_specs=(rows, rows, rows, rows, P(("ctx", "tp"), None, None)),
        out_specs=(rows, rows, P(("ctx", "tp"), "dp", None)),
        check_vma=False,
    )
```

```python
import jax
import jax.numpy as jnp
from jax import lax
from jax.experimental import pallas as pl
from jax.experimental.pallas import tpu as pltpu
from jax.sharding import PartitionSpec as P

grad_scale = 0.015625
PARTS = ((5,), (6, 5))
F32 = jnp.float32
BF16 = jnp.bfloat16
GROUP = ("ctx", "tp")


def call(body, outs, ins, name, flops=0, smem=0, scratch=(), in_hbm=(), out_hbm=(), limit=14):
    in_specs = [
        pl.BlockSpec(memory_space=pltpu.SMEM if i < smem else pltpu.HBM if i in in_hbm else pltpu.VMEM)
        for i in range(len(ins))
    ]
    return pl.pallas_call(
        body,
        out_shape=tuple(outs),
        in_specs=in_specs,
        out_specs=tuple(
            pl.BlockSpec(memory_space=pltpu.HBM if i in out_hbm else pltpu.VMEM) for i in range(len(outs))
        ),
        scratch_shapes=scratch,
        name=name,
        cost_estimate=pl.CostEstimate(flops=0, bytes_accessed=0, transcendentals=0),
        compiler_params=pltpu.CompilerParams(vmem_limit_bytes=limit * 2**20),
    )(*ins)


def like(shape, dtype=BF16):
    return jax.ShapeDtypeStruct(shape, dtype)


def iota(shape, axis):
    return lax.broadcasted_iota(jnp.int32, shape, axis)


def after(x, *others):
    return lax.optimization_barrier((x, others))[0]


def exchange(x, experts):
    shaped = x.reshape(experts, -1, x.shape[1])
    return lax.all_to_all(shaped, GROUP, split_axis=0, concat_axis=0, tiled=True).reshape(x.shape)


def slot_rows(ids, experts, capacity):
    choices, tokens = ids.shape
    named = [(iota((experts, tokens), 0) == ids[k : k + 1]).astype(F32) for k in range(choices)]
    before = (iota((tokens, tokens), 0) < iota((tokens, tokens), 1)).astype(BF16)
    earlier = jnp.dot(sum(named).astype(BF16), before, preferred_element_type=F32)
    slots = []
    for k in range(choices):
        rank = jnp.sum(named[k] * earlier, axis=0, keepdims=True)
        slots.append(ids[k : k + 1] * capacity + rank.astype(jnp.int32))
        earlier = earlier + named[k]
    return slots


def dispatch(ids, gates, grads, experts, capacity, widths):
    choices, tokens = ids.shape
    rows = experts * capacity

    def body(ids_hbm, gates_hbm, grads_hbm, *refs):
        *out_refs, ids_ref, gates_ref, grads_ref, sems = refs
        copies = [
            pltpu.make_async_copy(src, dst, sems.at[i])
            for i, (src, dst) in enumerate(
                ((ids_hbm, ids_ref), (gates_hbm, gates_ref), (grads_hbm, grads_ref))
            )
        ]
        for copy in copies:
            copy.start()
        copies[0].wait()
        slots = slot_rows(ids_ref[...], experts, capacity)
        copies[1].wait()
        pick = jnp.zeros((rows, tokens), F32)
        scale = jnp.zeros((rows, 1), F32)
        for k in range(choices):
            hit = iota((rows, tokens), 0) == slots[k]
            pick = pick + hit.astype(F32)
            scale = scale + jnp.sum(jnp.where(hit, gates_ref[k : k + 1, :], 0.0), axis=1, keepdims=True)
        pick = pick.astype(BF16)
        copies[2].wait()
        start = 0
        for ref, width in zip(out_refs, widths):
            chosen = jnp.dot(pick, grads_ref[:, start : start + width], preferred_element_type=F32)
            ref[...] = (chosen * scale).astype(BF16)
            start += width

    return call(
        body,
        [like((rows, w)) for w in widths],
        [ids, gates, grads],
        "dispatch",
        2 * rows * tokens * sum(widths),
        in_hbm=(0, 1, 2),
        limit=60,
        scratch=[
            pltpu.VMEM(ids.shape, ids.dtype),
            pltpu.VMEM(gates.shape, gates.dtype),
            pltpu.VMEM(grads.shape, grads.dtype),
            pltpu.SemaphoreType.DMA((3,)),
        ],
    )


def combine(ids, gates, returned, experts, capacity):
    choices, tokens = ids.shape
    rows, width = returned.shape

    def body(ids_ref, gates_ref, returned_ref, out_ref):
        slots = slot_rows(ids_ref[...], experts, capacity)
        same = iota((tokens, tokens), 0) == iota((tokens, tokens), 1)
        picks, scales = [], []
        for k in range(choices):
            slot = jnp.sum(jnp.where(same, slots[k], 0), axis=1, keepdims=True)
            picks.append((iota((tokens, rows), 1) == slot).astype(F32).astype(BF16))
            scales.append(jnp.sum(jnp.where(same, gates_ref[k : k + 1, :], 0.0), axis=1, keepdims=True))
        step = min(512, width)
        for start in range(0, width, step):
            block = returned_ref[:, start : start + step]
            out_ref[:, start : start + step] = sum(
                jnp.dot(p, block, preferred_element_type=F32) * s for p, s in zip(picks, scales)
            ).astype(BF16)

    return call(
        body,
        [like((tokens, width))],
        [ids, gates, returned],
        "combine",
        2 * choices * rows * tokens * width,
    )[0]


def expert_rows(rows, weight):
    width = weight.shape[1]
    step = min(512, width)

    def body(rows_ref, weight_ref, out_hbm, out_ref, sems):
        copies = []
        for i, start in enumerate(range(0, width, step)):
            columns = slice(start, start + step)
            out_ref[:, columns] = jnp.dot(
                rows_ref[...], weight_ref[:, columns], preferred_element_type=F32
            ).astype(BF16)
            copies.append(pltpu.make_async_copy(out_ref.at[:, columns], out_hbm.at[:, columns], sems.at[i]))
            copies[-1].start()
        for copy in copies:
            copy.wait()

    out = like((rows.shape[0], width))
    return call(
        body,
        [out],
        [rows, weight],
        "expert_rows",
        2 * rows.shape[0] * weight.size,
        out_hbm=(0,),
        limit=60,
        scratch=[pltpu.VMEM(out.shape, out.dtype), pltpu.SemaphoreType.DMA((width // step,))],
    )[0]


def grad_rows(pieces, weight):
    rows, hidden_units = pieces[0].shape[0], weight.shape[0]

    def body(weight_ref, *refs):
        *piece_refs, out_ref = refs
        total, start = None, 0
        for ref in piece_refs:
            width = ref.shape[1]
            part = lax.dot_general(
                ref[...],
                weight_ref[:, start : start + width],
                (((1,), (1,)), ((), ())),
                preferred_element_type=F32,
            )
            total = part if total is None else total + part
            start += width
        out_ref[...] = total.astype(BF16)

    return call(
        body,
        [like((rows, hidden_units))],
        [weight, *pieces],
        "grad_rows",
        2 * rows * weight.size,
    )[0]


def folded_part(spot, mine, theirs, piece, piece_theirs, stays):
    half, width = mine.shape[1] // 2, piece.shape[1]

    def body(spot_ref, mine_ref, theirs_ref, piece_ref, piece_theirs_ref, out_ref):
        which = spot_ref[0] if stays else 1 - spot_ref[0]
        columns = pl.ds(pl.multiple_of(which * half, half), half)
        out_ref[...] = sum(
            lax.dot_general(h[:, columns], p[...], (((0,), (0,)), ((), ())), preferred_element_type=F32)
            for h, p in ((mine_ref, piece_ref), (theirs_ref, piece_theirs_ref))
        ).astype(BF16)

    return call(
        body,
        [like((half, width))],
        [spot, mine, theirs, piece, piece_theirs],
        "kept_part" if stays else "given_part",
        4 * mine.shape[0] * half * width,
        smem=1,
    )[0]


def finish(spot, keep, got):
    half, width = keep.shape
    share = half // 2

    def body(spot_ref, keep_ref, got_ref, own_ref, give_ref):
        def rows(which):
            at = pl.ds(pl.multiple_of(which * share, share), share)
            return ((keep_ref[at, :].astype(F32) + got_ref[at, :].astype(F32)) * grad_scale).astype(BF16)

        give_ref[...] = rows(spot_ref[0])
        own_ref[...] = rows(1 - spot_ref[0])

    return call(body, [like((share, width))] * 2, [spot, keep, got], "finish", smem=1)


def shares(spot, own, handed):
    rows, width = own[0].shape[0], sum(x.shape[1] for x in own)

    def body(spot_ref, *refs):
        *in_refs, out_ref = refs
        at_end, start = spot_ref[1] != 0, 0
        for own_ref, handed_ref in zip(in_refs[: len(own)], in_refs[len(own) :]):
            columns = slice(start, start + own_ref.shape[1])
            out_ref[:, columns] = jnp.where(at_end, handed_ref[...], own_ref[...])
            start += own_ref.shape[1]

    return call(body, [like((rows, width))], [spot, *own, *handed], "shares", smem=1)[0]


def local(hidden, grad_output, expert_ids, gate_weights, w_down):
    replicas = lax.axis_size("dp")
    experts = lax.axis_size("ctx") * lax.axis_size("tp")
    capacity = hidden.shape[0] // experts
    width = grad_output.shape[1]
    weight = w_down[0]
    ids, gates = expert_ids.T, gate_weights.T
    widths = [[p * width // 16 for p in cuts] for cuts in PARTS]
    line = replicas == 4
    fold, swap, back = [(0, 1), (3, 2)], [(1, 2), (2, 1)], [(1, 0), (2, 3)]

    theirs = lax.ppermute(hidden, "dp", fold) if line else hidden
    outgoing = dispatch(ids, gates, grad_output, experts, capacity, [sum(w) for w in widths])
    expert_out = expert_rows(hidden, weight)
    if not line:
        pieces = [exchange(x, experts) for x in outgoing]
        returned = exchange(expert_out, experts)
        incoming = jnp.concatenate(pieces, axis=1)
        part = lax.dot_general(hidden, incoming, (((0,), (0,)), ((), ())), preferred_element_type=F32)
        summed = lax.psum_scatter(part.astype(BF16), "dp", scatter_dimension=0, tiled=True)
        grad_down = (summed.astype(F32) * grad_scale).astype(BF16)
        combined = combine(ids, gates, returned, experts, capacity)
        return (combined, grad_rows(pieces, weight), grad_down[None])

    place = lax.axis_index("dp")
    at_end = (place == 0) | (place == replicas - 1)
    spot = jnp.stack([(2 * place >= replicas).astype(jnp.int32), at_end.astype(jnp.int32)])

    first = exchange(outgoing[0], experts)
    pieces, folded = [first], [lax.ppermute(first, "dp", fold)]
    give = folded_part(spot, hidden, theirs, pieces[0], folded[0], False)
    gives = [give]
    arrived = after(exchange(after(outgoing[1], expert_out, theirs), experts), give)
    start = 0
    for cut in widths[1]:
        pieces.append(arrived[:, start : start + cut])
        folded.append(lax.ppermute(pieces[-1], "dp", fold))
        start += cut
    last = len(pieces) - 1
    got = [lax.ppermute(give, "dp", swap)]
    returned = exchange(after(expert_out, pieces[-1], give), experts)
    folded[1] = after(folded[1], got[0])
    for i in range(1, last):
        give = folded_part(spot, hidden, theirs, pieces[i], folded[i], False)
        gives.append(give)
        got.append(lax.ppermute(give, "dp", swap))

    early = list(after(tuple(pieces), gives[-1]))
    grad_hidden = grad_rows(early, weight)
    keeps = [folded_part(spot, hidden, theirs, early[0], folded[0], True)]
    folded[last] = after(folded[last], grad_hidden, keeps[0])
    give = folded_part(spot, hidden, theirs, pieces[last], folded[last], False)
    gives.append(give)
    got.append(lax.ppermute(give, "dp", swap))

    late = after(tuple(pieces), give)
    got[:last] = after(tuple(got[:last]), give)
    keeps += [folded_part(spot, hidden, theirs, late[i], folded[i], True) for i in range(1, last + 1)]
    formed, handed = [], []
    for i in range(last + 1):
        own, give = finish(spot, keeps[i], got[i])
        formed.append(own)
        handed.append(lax.ppermute(give, "dp", back))
        if i < last:
            got[-1] = after(got[-1], handed[-1] if i < last - 1 else formed[-1])
    combined = combine(ids, gates, returned, experts, capacity)
    grad_down = shares(spot, formed, handed)
    return (combined, grad_hidden, grad_down[None])


def solution(mesh):
    rows = P(("dp", "ctx", "tp"), None)
    return jax.shard_map(
        local,
        mesh=mesh,
        in_specs=(rows, rows, rows, rows, P(("ctx", "tp"), None, None)),
        out_specs=(rows, rows, P(("ctx", "tp"), "dp", None)),
        check_vma=False,
    )
```

```python
import jax
import jax.numpy as jnp
from jax import lax
from jax.experimental import pallas as pl
from jax.experimental.pallas import tpu as pltpu
from jax.sharding import PartitionSpec as P

grad_scale = 0.015625
PARTS = ((5,), (6, 5))
F32 = jnp.float32
BF16 = jnp.bfloat16
GROUP = ("ctx", "tp")


def call(body, outs, ins, name, flops=0, smem=0, scratch=(), in_hbm=(), out_hbm=(), limit=14):
    in_specs = [
        pl.BlockSpec(memory_space=pltpu.SMEM if i < smem else pltpu.HBM if i in in_hbm else pltpu.VMEM)
        for i in range(len(ins))
    ]
    return pl.pallas_call(
        body,
        out_shape=tuple(outs),
        in_specs=in_specs,
        out_specs=tuple(
            pl.BlockSpec(memory_space=pltpu.HBM if i in out_hbm else pltpu.VMEM) for i in range(len(outs))
        ),
        scratch_shapes=scratch,
        name=name,
        cost_estimate=pl.CostEstimate(flops=0, bytes_accessed=0, transcendentals=0),
        compiler_params=pltpu.CompilerParams(vmem_limit_bytes=limit * 2**20),
    )(*ins)


def like(shape, dtype=BF16):
    return jax.ShapeDtypeStruct(shape, dtype)


def iota(shape, axis):
    return lax.broadcasted_iota(jnp.int32, shape, axis)


def after(x, *others):
    return lax.optimization_barrier((x, others))[0]


def exchange(x, experts):
    shaped = x.reshape(experts, -1, x.shape[1])
    return lax.all_to_all(shaped, GROUP, split_axis=0, concat_axis=0, tiled=True).reshape(x.shape)


def slot_rows(ids, experts, capacity):
    choices, tokens = ids.shape
    named = [(iota((experts, tokens), 0) == ids[k : k + 1]).astype(F32) for k in range(choices)]
    before = (iota((tokens, tokens), 0) < iota((tokens, tokens), 1)).astype(BF16)
    earlier = jnp.dot(sum(named).astype(BF16), before, preferred_element_type=F32)
    slots = []
    for k in range(choices):
        rank = jnp.sum(named[k] * earlier, axis=0, keepdims=True)
        slots.append(ids[k : k + 1] * capacity + rank.astype(jnp.int32))
        earlier = earlier + named[k]
    return slots


def dispatch(ids, gates, grads, experts, capacity, widths):
    choices, tokens = ids.shape
    rows = experts * capacity

    def body(ids_hbm, gates_hbm, grads_hbm, *refs):
        *out_refs, ids_ref, gates_ref, grads_ref, sems = refs
        copies = [
            pltpu.make_async_copy(src, dst, sems.at[i])
            for i, (src, dst) in enumerate(
                ((ids_hbm, ids_ref), (gates_hbm, gates_ref), (grads_hbm, grads_ref))
            )
        ]
        for copy in copies:
            copy.start()
        copies[0].wait()
        slots = slot_rows(ids_ref[...], experts, capacity)
        copies[1].wait()
        pick = jnp.zeros((rows, tokens), F32)
        scale = jnp.zeros((rows, 1), F32)
        for k in range(choices):
            hit = iota((rows, tokens), 0) == slots[k]
            pick = pick + hit.astype(F32)
            scale = scale + jnp.sum(jnp.where(hit, gates_ref[k : k + 1, :], 0.0), axis=1, keepdims=True)
        pick = pick.astype(BF16)
        copies[2].wait()
        start = 0
        for ref, width in zip(out_refs, widths):
            chosen = jnp.dot(pick, grads_ref[:, start : start + width], preferred_element_type=F32)
            ref[...] = (chosen * scale).astype(BF16)
            start += width

    return call(
        body,
        [like((rows, w)) for w in widths],
        [ids, gates, grads],
        "dispatch",
        2 * rows * tokens * sum(widths),
        in_hbm=(0, 1, 2),
        limit=60,
        scratch=[
            pltpu.VMEM(ids.shape, ids.dtype),
            pltpu.VMEM(gates.shape, gates.dtype),
            pltpu.VMEM(grads.shape, grads.dtype),
            pltpu.SemaphoreType.DMA((3,)),
        ],
    )


def combine(ids, gates, returned, experts, capacity):
    choices, tokens = ids.shape
    rows, width = returned.shape

    def body(ids_ref, gates_ref, returned_ref, out_ref):
        slots = slot_rows(ids_ref[...], experts, capacity)
        same = iota((tokens, tokens), 0) == iota((tokens, tokens), 1)
        picks, scales = [], []
        for k in range(choices):
            slot = jnp.sum(jnp.where(same, slots[k], 0), axis=1, keepdims=True)
            picks.append((iota((tokens, rows), 1) == slot).astype(F32).astype(BF16))
            scales.append(jnp.sum(jnp.where(same, gates_ref[k : k + 1, :], 0.0), axis=1, keepdims=True))
        step = min(512, width)
        for start in range(0, width, step):
            block = returned_ref[:, start : start + step]
            out_ref[:, start : start + step] = sum(
                jnp.dot(p, block, preferred_element_type=F32) * s for p, s in zip(picks, scales)
            ).astype(BF16)

    return call(
        body,
        [like((tokens, width))],
        [ids, gates, returned],
        "combine",
        2 * choices * rows * tokens * width,
    )[0]


def expert_rows(rows, weight):
    width = weight.shape[1]
    step = min(512, width)

    def body(rows_ref, weight_ref, out_hbm, out_ref, sems):
        copies = []
        for i, start in enumerate(range(0, width, step)):
            columns = slice(start, start + step)
            out_ref[:, columns] = jnp.dot(
                rows_ref[...], weight_ref[:, columns], preferred_element_type=F32
            ).astype(BF16)
            copies.append(pltpu.make_async_copy(out_ref.at[:, columns], out_hbm.at[:, columns], sems.at[i]))
            copies[-1].start()
        for copy in copies:
            copy.wait()

    out = like((rows.shape[0], width))
    return call(
        body,
        [out],
        [rows, weight],
        "expert_rows",
        2 * rows.shape[0] * weight.size,
        out_hbm=(0,),
        limit=60,
        scratch=[pltpu.VMEM(out.shape, out.dtype), pltpu.SemaphoreType.DMA((width // step,))],
    )[0]


def grad_rows(pieces, weight):
    rows, hidden_units = pieces[0].shape[0], weight.shape[0]

    def body(weight_ref, *refs):
        *piece_refs, out_ref = refs
        total, start = None, 0
        for ref in piece_refs:
            width = ref.shape[1]
            part = lax.dot_general(
                ref[...],
                weight_ref[:, start : start + width],
                (((1,), (1,)), ((), ())),
                preferred_element_type=F32,
            )
            total = part if total is None else total + part
            start += width
        out_ref[...] = total.astype(BF16)

    return call(
        body,
        [like((rows, hidden_units))],
        [weight, *pieces],
        "grad_rows",
        2 * rows * weight.size,
    )[0]


def folded_part(spot, mine, theirs, piece, piece_theirs, stays):
    half, width = mine.shape[1] // 2, piece.shape[1]

    def body(spot_ref, mine_ref, theirs_ref, piece_ref, piece_theirs_ref, out_ref):
        which = spot_ref[0] if stays else 1 - spot_ref[0]
        columns = pl.ds(pl.multiple_of(which * half, half), half)
        out_ref[...] = sum(
            lax.dot_general(h[:, columns], p[...], (((0,), (0,)), ((), ())), preferred_element_type=F32)
            for h, p in ((mine_ref, piece_ref), (theirs_ref, piece_theirs_ref))
        ).astype(BF16)

    return call(
        body,
        [like((half, width))],
        [spot, mine, theirs, piece, piece_theirs],
        "kept_part" if stays else "given_part",
        4 * mine.shape[0] * half * width,
        smem=1,
    )[0]


def finish(spot, keep, got):
    half, width = keep.shape
    share = half // 2

    def body(spot_ref, keep_ref, got_ref, own_ref, give_ref):
        def rows(which):
            at = pl.ds(pl.multiple_of(which * share, share), share)
            return ((keep_ref[at, :].astype(F32) + got_ref[at, :].astype(F32)) * grad_scale).astype(BF16)

        give_ref[...] = rows(spot_ref[0])
        own_ref[...] = rows(1 - spot_ref[0])

    return call(body, [like((share, width))] * 2, [spot, keep, got], "finish", smem=1)


def shares(spot, own, handed):
    rows, width = own[0].shape[0], sum(x.shape[1] for x in own)

    def body(spot_ref, *refs):
        *in_refs, out_ref = refs
        at_end, start = spot_ref[1] != 0, 0
        for own_ref, handed_ref in zip(in_refs[: len(own)], in_refs[len(own) :]):
            columns = slice(start, start + own_ref.shape[1])
            out_ref[:, columns] = jnp.where(at_end, handed_ref[...], own_ref[...])
            start += own_ref.shape[1]

    return call(body, [like((rows, width))], [spot, *own, *handed], "shares", smem=1)[0]


def local(hidden, grad_output, expert_ids, gate_weights, w_down):
    replicas = lax.axis_size("dp")
    experts = lax.axis_size("ctx") * lax.axis_size("tp")
    capacity = hidden.shape[0] // experts
    width = grad_output.shape[1]
    weight = w_down[0]
    ids, gates = expert_ids.T, gate_weights.T
    widths = [[p * width // 16 for p in cuts] for cuts in PARTS]
    line = replicas == 4
    fold, swap, back = [(0, 1), (3, 2)], [(1, 2), (2, 1)], [(1, 0), (2, 3)]

    theirs = lax.ppermute(hidden, "dp", fold) if line else hidden
    outgoing = dispatch(ids, gates, grad_output, experts, capacity, [sum(w) for w in widths])
    expert_out = expert_rows(hidden, weight)
    if not line:
        pieces = [exchange(x, experts) for x in outgoing]
        returned = exchange(expert_out, experts)
        incoming = jnp.concatenate(pieces, axis=1)
        part = lax.dot_general(hidden, incoming, (((0,), (0,)), ((), ())), preferred_element_type=F32)
        summed = lax.psum_scatter(part.astype(BF16), "dp", scatter_dimension=0, tiled=True)
        grad_down = (summed.astype(F32) * grad_scale).astype(BF16)
        combined = combine(ids, gates, returned, experts, capacity)
        return (combined, grad_rows(pieces, weight), grad_down[None])

    place = lax.axis_index("dp")
    at_end = (place == 0) | (place == replicas - 1)
    spot = jnp.stack([(2 * place >= replicas).astype(jnp.int32), at_end.astype(jnp.int32)])

    first = exchange(outgoing[0], experts)
    pieces, folded = [first], [lax.ppermute(first, "dp", fold)]
    give = folded_part(spot, hidden, theirs, pieces[0], folded[0], False)
    gives = [give]
    arrived = after(exchange(after(outgoing[1], expert_out, theirs), experts), give)
    start = 0
    for cut in widths[1]:
        pieces.append(arrived[:, start : start + cut])
        folded.append(lax.ppermute(pieces[-1], "dp", fold))
        start += cut
    last = len(pieces) - 1
    got = [lax.ppermute(give, "dp", swap)]
    returned = exchange(after(expert_out, pieces[-1], give), experts)
    folded[1] = after(folded[1], got[0])
    for i in range(1, last):
        give = folded_part(spot, hidden, theirs, pieces[i], folded[i], False)
        gives.append(give)
        got.append(lax.ppermute(give, "dp", swap))

    early = list(after(tuple(pieces), gives[-1]))
    grad_hidden = grad_rows(early, weight)
    keeps = [folded_part(spot, hidden, theirs, early[0], folded[0], True)]
    folded[last] = after(folded[last], grad_hidden, keeps[0])
    give = folded_part(spot, hidden, theirs, pieces[last], folded[last], False)
    gives.append(give)
    got.append(lax.ppermute(give, "dp", swap))

    late = after(tuple(pieces), give)
    got[:last] = after(tuple(got[:last]), give)
    keeps += [folded_part(spot, hidden, theirs, late[i], folded[i], True) for i in range(1, last + 1)]
    formed, handed = [], []
    for i in range(last + 1):
        own, give = finish(spot, keeps[i], got[i])
        formed.append(own)
        handed.append(lax.ppermute(give, "dp", back))
        if i < last:
            got[-1] = after(got[-1], formed[-1])
    combined = combine(ids, gates, returned, experts, capacity)
    grad_down = shares(spot, formed, handed)
    return (combined, grad_hidden, grad_down[None])


def solution(mesh):
    rows = P(("dp", "ctx", "tp"), None)
    return jax.shard_map(
        local,
        mesh=mesh,
        in_specs=(rows, rows, rows, rows, P(("ctx", "tp"), None, None)),
        out_specs=(rows, rows, P(("ctx", "tp"), "dp", None)),
        check_vma=False,
    )
```
